256 devices in a mesh: ctx: 32 (over z, x_hi, core), tp: 8 (over x_lo, y).
Axes of the slice: x: 4 (x_hi: 2, x_lo: 2; x = x_hi * 2 + x_lo), y: 4, z: 8, core: 2. Of those that a mesh axis runs over, the one named last changes fastest.
Arguments:
- queries: bfloat16 [1, 8192, 8192], P(None, 'ctx', 'tp'), may hold values from -8 to 8
- keys: bfloat16 [1, 8192, 1024], P(None, 'ctx', 'tp'), may hold values from -5 to 5
- values: bfloat16 [1, 8192, 1024], P(None, 'ctx', 'tp'), may hold values from -6 to 6
Outputs:
- attended: bfloat16 [1, 8192, 8192], P(None, ('ctx', 'tp'))
The draws below stay inside these ranges and needn't reach their ends.
All inputs are finite; a program needn't handle non-finite values.
Results may differ from the reference program's by a relative error of at most 0.0075.
Values may be sent and summed in bfloat16 or wider, within the bound.
A program may use at most 64 MiB of HBM per device.

```python
import jax
import jax.numpy as jnp
from jax import lax

HEADS = 64
KVH = 8
HD = 128
SEQ = 8192
SEQS = 1


def draw_pair(key):
    base = jax.random.fold_in(key, 11)
    query_key, keys_key = jax.random.split(base, 2)
    query_shape = (SEQS, SEQ, HEADS * HD)
    keys_shape = (SEQS, SEQ, KVH * HD)
    query_draw = jnp.clip(2.0 * jax.random.normal(query_key, query_shape, jnp.float32), -8.0, 8.0)
    keys_draw = jnp.clip(jax.random.normal(keys_key, keys_shape, jnp.float32), -5.0, 5.0)
    return (query_draw, keys_draw)


def draw_queries(key, part):
    return draw_pair(key)[0].astype(jnp.bfloat16)


def draw_keys(key, part):
    return draw_pair(key)[1].astype(jnp.bfloat16)


def shard_levels(key, dims, cuts, least, largest):
    def one(dim, blocks):
        draws = jax.random.uniform(jax.random.fold_in(jax.random.fold_in(key, 6), dim), (blocks,), jnp.float32, least / len(cuts), largest / len(cuts))
        return jnp.repeat(jnp.exp(draws), dims[dim] // blocks).reshape((-1,) + (1,) * (len(dims) - dim - 1))

    factor_of = one(*cuts[0])
    for cut in cuts[1:]:
        factor_of = factor_of * one(*cut)
    return factor_of


def noise(stream_key, dims, scale, limit, cuts=(), held_as=jnp.bfloat16):
    factor_of = shard_levels(stream_key, dims, cuts, -0.22, 0.18) if cuts else 1.0
    array = jax.random.normal(stream_key, dims, jnp.float32) * scale * factor_of
    return jnp.minimum(jnp.maximum(array, -limit), limit).astype(held_as)


def setup_inputs(seed: int = 0) -> dict:
    splits = jax.random.split(jax.random.key(seed), 4)
    queries = draw_queries(jax.random.fold_in(splits[3], 71), 0)
    keys = draw_keys(jax.random.fold_in(splits[3], 71), 0)
    values = noise(splits[2], (SEQS, SEQ, KVH * HD), 1.0, 6.0, ((1, 32), (2, 8)))
    return dict(queries=queries, keys=keys, values=values)


def reference(queries, keys, values):
    group_size = HEADS // KVH
    block_rows = min(SEQ, 512)
    block_count = SEQ // block_rows
    score_scale = HD ** -0.5
    positions = jnp.arange(SEQ, dtype=jnp.int32)
    results = []
    for seq_index in range(SEQS):
        key_all = keys[seq_index].astype(jnp.float32).reshape(SEQ, KVH, HD)
        value_all = values[seq_index].astype(jnp.float32).reshape(SEQ, KVH, HD)
        query_all = queries[seq_index].astype(jnp.float32).reshape(SEQ, KVH, group_size, HD)
        head_outputs = []
        for head_index in range(KVH):
            key_head = key_all[:, head_index]
            value_head = value_all[:, head_index]
            query_blocks = query_all[:, head_index].reshape(block_count, block_rows, group_size, HD)
            block_starts = jnp.arange(block_count, dtype=jnp.int32) * block_rows

            def attend(inputs, key_head=key_head, value_head=value_head):
                query_block, block_start = inputs
                scores = jnp.einsum("qhd,rd->qhr", query_block, key_head) * score_scale
                query_pos = block_start + jnp.arange(block_rows, dtype=jnp.int32)
                visible = query_pos[:, None, None] >= positions[None, None, :]
                masked = jnp.where(visible, scores, -1e30)
                rowmax = jnp.max(masked, axis=-1, keepdims=True)
                raised = jnp.where(visible, jnp.exp(masked - rowmax), 0.0)
                denominator = jnp.sum(raised, axis=-1, keepdims=True)
                weights = raised.astype(jnp.bfloat16)
                summed = jnp.einsum("qhr,rd->qhd", weights.astype(jnp.float32), value_head)
                return (summed / denominator).astype(jnp.bfloat16)

            attended_head = lax.map(attend, (query_blocks, block_starts))
            head_outputs.append(attended_head.reshape(SEQ, group_size, HD))
        stacked = jnp.stack(head_outputs, axis=1)
        results.append(stacked.reshape(SEQ, HEADS * HD))
    return jnp.stack(results, axis=0)
```

```python
import math

import jax
import jax.numpy as jnp
from jax import lax
from jax.experimental import pallas as pl
from jax.experimental.pallas import tpu as pltpu
from jax.sharding import PartitionSpec as P

HD = 128
BLOCK = 1024
UNROLL = 4
SCALE = math.log2(math.e) / math.sqrt(HD)


def flash(q_ref, k_ref, v_ref, out_ref, best_ref, acc_ref):
    rows, width = q_ref.shape
    heads = width // HD
    row_start = lax.axis_index("ctx") * rows
    best_ref[...] = jnp.full_like(best_ref, -1e30)
    acc_ref[...] = jnp.zeros_like(acc_ref)

    def block(index, masked):
        start = pl.multiple_of(index * BLOCK, BLOCK)
        key = k_ref[pl.ds(start, BLOCK), :]
        value = jnp.concatenate(
            [v_ref[pl.ds(start, BLOCK), :], jnp.ones((BLOCK, HD), jnp.bfloat16)], axis=1
        )

        def head_group(group, carry):
            for u in range(UNROLL):
                head = group * UNROLL + u
                q = q_ref[:, pl.ds(pl.multiple_of(head * HD, HD), HD)]
                s = lax.dot_general(
                    q, key, (((1,), (1,)), ((), ())), preferred_element_type=jnp.float32
                )
                if masked:
                    row = row_start - start + lax.broadcasted_iota(jnp.int32, s.shape, 0)
                    col = lax.broadcasted_iota(jnp.int32, s.shape, 1)
                    s = jnp.where(col <= row, s, -1e30)
                old = best_ref[head]
                new = jnp.maximum(old, jnp.max(s, axis=1, keepdims=True))
                fade = jnp.exp2((old - new) * SCALE)
                p = jnp.exp2((s - new[:, :1]) * SCALE).astype(jnp.bfloat16)
                pv = jnp.dot(p, value, preferred_element_type=jnp.float32)
                acc_ref[head] = acc_ref[head] * jnp.concatenate([fade, fade], axis=1) + pv
                best_ref[head] = new
            return carry

        lax.fori_loop(0, heads // UNROLL, head_group, 0)

    last = row_start // BLOCK
    block(last, True)

    def full(index, carry):
        block(index, False)
        return carry

    lax.fori_loop(0, last, full, 0)
    for head in range(heads):
        acc = acc_ref[head]
        out_ref[:, head * HD : (head + 1) * HD] = (acc[:, :HD] / acc[:, HD:]).astype(jnp.bfloat16)


def local(queries, keys, values):
    _, rows, width = queries.shape
    heads = width // HD
    key_all = lax.all_gather(keys[0], "ctx", axis=0, tiled=True)
    value_all = lax.all_gather(values[0], "ctx", axis=0, tiled=True)
    attended = pl.pallas_call(
        flash,
        out_shape=jax.ShapeDtypeStruct((rows, width), jnp.bfloat16),
        in_specs=[pl.BlockSpec(memory_space=pltpu.VMEM)] * 3,
        out_specs=pl.BlockSpec(memory_space=pltpu.VMEM),
        scratch_shapes=[
            pltpu.VMEM((heads, rows, HD), jnp.float32),
            pltpu.VMEM((heads, rows, 2 * HD), jnp.float32),
        ],
        compiler_params=pltpu.CompilerParams(vmem_limit_bytes=48 * 2**20),
        name="flash",
    )(queries[0], key_all, value_all)
    return lax.all_to_all(attended[None], "tp", split_axis=1, concat_axis=2, tiled=True)


def solution(mesh):
    in_specs = (P(None, "ctx", "tp"), P(None, "ctx", "tp"), P(None, "ctx", "tp"))
    out_specs = P(None, ("ctx", "tp"), None)
    return jax.shard_map(local, mesh=mesh, in_specs=in_specs, out_specs=out_specs, check_vma=False)
```

```python
import functools
import math

import jax
import jax.numpy as jnp
from jax import lax
from jax.experimental import pallas as pl
from jax.experimental.pallas import tpu as pltpu
from jax.sharding import PartitionSpec as P

HD = 128
UNROLL = 4
SCALE = math.log2(math.e) / math.sqrt(HD)
MESH = pl.DeviceIdType.MESH

PLANE = 4
UP, DOWN = 0, 1
NEAR, FAR = 0, 1


def kernel(
    planes,
    peers,
    q_hbm,
    k_hbm,
    v_hbm,
    out_ref,
    q_ref,
    kv_ref,
    best_ref,
    acc_ref,
    stage_ref,
    load_sem,
    x_sem,
    ring_send,
    ring_recv,
    core_send,
    core_recv,
    out_send,
    out_recv,
    own_sem,
):
    rows, width = q_ref.shape
    block_rows = PLANE * rows
    heads = width // HD
    groups = heads // UNROLL
    part = rows // peers
    reach = planes // 2
    me = lax.axis_index("ctx")
    tp = lax.axis_index("tp")
    z, x, core = me // PLANE, (me // 2) % 2, me % 2

    def slot(plane, col, c):
        return plane * PLANE + (x if col == NEAR else 1 - x) * 2 + c

    def beside(d, step):
        return lax.rem(z + planes - step if d == UP else z + step, planes)

    neighbour = (
        lax.rem(z + 1, planes) * PLANE + x * 2 + core,
        lax.rem(z + planes - 1, planes) * PLANE + x * 2 + core,
    )
    x_partner = z * PLANE + (1 - x) * 2 + core
    core_partner = z * PLANE + x * 2 + 1 - core

    def last(d, col):
        return reach if (d == UP) == (col == NEAR) else reach - 1

    def remote(index, send, recv, target):
        return pltpu.make_async_remote_copy(
            src_ref=kv_ref.at[index],
            dst_ref=kv_ref.at[index],
            send_sem=send,
            recv_sem=recv,
            device_id={"ctx": target},
            device_id_type=MESH,
        )

    def hop(d, col, step):
        return remote(
            slot(beside(d, step), col, core),
            ring_send.at[d, col, step],
            ring_recv.at[d, col, step + 1],
            neighbour[d],
        )

    def across(d, col, step, c):
        return remote(
            slot(beside(d, step), col, c),
            core_send.at[d, col, step],
            core_recv.at[d, col, step],
            core_partner,
        )

    def arrive(d, col, step):
        remote(
            slot(beside(d, step), col, core),
            ring_send.at[d, col, step],
            ring_recv.at[d, col, step],
            neighbour[d],
        ).wait_recv()

        @pl.when(step < last(d, col))
        def _():
            hop(d, col, step).start()

        across(d, col, step, core).start()

    def arrive_both(col, step):
        for d in (UP, DOWN):

            @pl.when(step <= last(d, col))
            def _():
                arrive(d, col, step)

    loads = [
        pltpu.make_async_copy(k_hbm, kv_ref.at[me, 0], load_sem.at[0]),
        pltpu.make_async_copy(v_hbm, kv_ref.at[me, 1], load_sem.at[1]),
        pltpu.make_async_copy(q_hbm, q_ref, load_sem.at[2]),
    ]
    for load in loads:
        load.start()
    barrier = pltpu.get_barrier_semaphore()
    for target in (*neighbour, x_partner, core_partner):
        pl.semaphore_signal(barrier, inc=1, device_id={"ctx": target}, device_id_type=MESH)
    for j in range(1, peers):
        pl.semaphore_signal(
            barrier, inc=1, device_id={"tp": lax.rem(tp + j, peers)}, device_id_type=MESH
        )
    loads[0].wait()
    loads[1].wait()
    pl.semaphore_wait(barrier, 4 + peers - 1)

    x_copy = remote(me, x_sem.at[0], x_sem.at[1], x_partner)
    x_copy.start()
    for d in (UP, DOWN):
        hop(d, NEAR, 0).start()
    across(UP, NEAR, 0, core).start()
    best_ref[...] = jnp.full_like(best_ref, -1e30)
    acc_ref[...] = jnp.zeros_like(acc_ref)
    arrive_both(NEAR, 1)
    remote(x_partner, x_sem.at[0], x_sem.at[1], x_partner).wait_recv()
    for d in (UP, DOWN):
        hop(d, FAR, 0).start()
    across(UP, FAR, 0, core).start()
    across(UP, NEAR, 0, 1 - core).wait_recv()
    across(UP, FAR, 0, 1 - core).wait_recv()
    loads[2].wait()

    def attend(plane, group, masked):
        held = kv_ref.at[pl.ds(plane * PLANE, PLANE)]
        key = held[:, 0].reshape(block_rows, HD)
        value = jnp.concatenate(
            [held[:, 1].reshape(block_rows, HD), jnp.ones((block_rows, HD), jnp.bfloat16)], axis=1
        )
        for u in range(UNROLL):
            head = group * UNROLL + u
            q = q_ref[:, pl.ds(pl.multiple_of(head * HD, HD), HD)]
            s = lax.dot_general(q, key, (((1,), (1,)), ((), ())), preferred_element_type=jnp.float32)
            if masked:
                row = (me - plane * PLANE) * rows + lax.broadcasted_iota(jnp.int32, s.shape, 0)
                col = lax.broadcasted_iota(jnp.int32, s.shape, 1)
                s = jnp.where(col <= row, s, -1e30)
            old = best_ref[head]
            new = jnp.maximum(old, jnp.max(s, axis=1, keepdims=True))
            fade = jnp.exp2((old - new) * SCALE)
            p = jnp.exp2((s - new[:, :1]) * SCALE).astype(jnp.bfloat16)
            pv = jnp.dot(p, value, preferred_element_type=jnp.float32)
            acc_ref[head] = acc_ref[head] * jnp.concatenate([fade, fade], axis=1) + pv
            best_ref[head] = new

    def own(group, carry):
        @pl.when(group == 0)
        def _():
            arrive_both(NEAR, 2)

        @pl.when(group == groups - 1)
        def _():
            arrive_both(FAR, 1)

        attend(z, group, True)
        return carry

    lax.fori_loop(0, groups, own, 0)

    def attend_step(step, carry):
        def attend_side(d, carry):
            @pl.when(d == 0)
            def _():
                arrive_both(NEAR, step + 2)
                for col in (NEAR, FAR):
                    across(UP, col, step, 1 - core).wait_recv()

            @pl.when(d == 1)
            def _():
                arrive_both(FAR, step + 1)
                for col in (NEAR, FAR):
                    across(DOWN, col, step, 1 - core).wait_recv()

            plane = lax.rem(z + planes + (2 * d - 1) * step, planes)

            @pl.when(plane < z)
            def _():
                def each(group, carry):
                    attend(plane, group, False)
                    return carry

                lax.fori_loop(0, groups, each, 0)

            return carry

        return lax.fori_loop(0, 2, attend_side, carry)

    lax.fori_loop(1, reach, attend_step, 0)
    across(UP, NEAR, reach, 1 - core).wait_recv()
    across(DOWN, FAR, reach, 1 - core).wait_recv()

    cut = UNROLL * HD

    def give(group, j, to, column):
        return pltpu.make_async_remote_copy(
            src_ref=stage_ref.at[
                pl.ds(pl.multiple_of(to * part, part), part),
                pl.ds(pl.multiple_of(group * cut, cut), cut),
            ],
            dst_ref=out_ref.at[:, pl.ds(pl.multiple_of(column * width + group * cut, cut), cut)],
            send_sem=out_send.at[group, j],
            recv_sem=out_recv.at[group, j],
            device_id={"tp": to},
            device_id_type=MESH,
        )

    def keep(group):
        return pltpu.make_async_copy(
            stage_ref.at[
                pl.ds(pl.multiple_of(tp * part, part), part),
                pl.ds(pl.multiple_of(group * cut, cut), cut),
            ],
            out_ref.at[:, pl.ds(pl.multiple_of(tp * width + group * cut, cut), cut)],
            own_sem.at[group],
        )

    def finish(group, carry):
        @pl.when(z >= reach)
        def _():
            attend(z - reach, group, False)

        for u in range(UNROLL):
            head = group * UNROLL + u
            acc = acc_ref[head]
            stage_ref[:, pl.ds(pl.multiple_of(head * HD, HD), HD)] = (
                acc[:, :HD] / acc[:, HD:]
            ).astype(jnp.bfloat16)
        for j in range(1, peers):
            give(group, j, lax.rem(tp + j, peers), tp).start()
        keep(group).start()
        return carry

    lax.fori_loop(0, groups, finish, 0)

    x_copy.wait_send()
    for d in (UP, DOWN):
        for col in (NEAR, FAR):
            for step in range(last(d, col) + 1):
                if step < last(d, col):
                    hop(d, col, step).wait_send()
                if step > 0 or d == UP:
                    across(d, col, step, core).wait_send()
    for group in range(groups):
        for j in range(1, peers):
            copy = give(group, j, lax.rem(tp + j, peers), lax.rem(tp + peers - j, peers))
            copy.wait_send()
            copy.wait_recv()
        keep(group).wait()


def local(planes, peers, queries, keys, values):
    _, rows, width = queries.shape
    heads = width // HD
    groups = heads // UNROLL
    steps = planes // 2 + 1
    dma = pltpu.SemaphoreType.DMA
    out = pl.pallas_call(
        functools.partial(kernel, planes, peers),
        out_shape=jax.ShapeDtypeStruct((rows // peers, width * peers), jnp.bfloat16),
        in_specs=[pl.BlockSpec(memory_space=pl.ANY)] * 3,
        out_specs=pl.BlockSpec(memory_space=pltpu.VMEM),
        scratch_shapes=[
            pltpu.VMEM((rows, width), jnp.bfloat16),
            pltpu.VMEM((planes * PLANE, 2, rows, HD), jnp.bfloat16),
            pltpu.VMEM((heads, rows, HD), jnp.float32),
            pltpu.VMEM((heads, rows, 2 * HD), jnp.float32),
            pltpu.VMEM((rows, width), jnp.bfloat16),
            dma((3,)),
            dma((2,)),
            dma((2, 2, steps)),
            dma((2, 2, steps)),
            dma((2, 2, steps)),
            dma((2, 2, steps)),
            dma((groups, peers)),
            dma((groups, peers)),
            dma((groups,)),
        ],
        compiler_params=pltpu.CompilerParams(
            vmem_limit_bytes=48 * 2**20, collective_id=0, has_side_effects=True
        ),
        name="ring_attention",
    )(queries[0], keys[0], values[0])
    return out[None]


def solution(mesh):
    in_specs = (P(None, "ctx", "tp"), P(None, "ctx", "tp"), P(None, "ctx", "tp"))
    out_specs = P(None, ("ctx", "tp"), None)
    planes, peers = mesh.shape["ctx"] // PLANE, mesh.shape["tp"]
    return jax.shard_map(
        functools.partial(local, planes, peers),
        mesh=mesh,
        in_specs=in_specs,
        out_specs=out_specs,
        check_vma=False,
    )
```

```python
import functools
import math

import jax
import jax.numpy as jnp
from jax import lax
from jax.experimental import pallas as pl
from jax.experimental.pallas import tpu as pltpu
from jax.sharding import PartitionSpec as P

HD = 128
UNROLL = 4
SCALE = math.log2(math.e) / math.sqrt(HD)
MESH = pl.DeviceIdType.MESH

PLANE = 4
UP, DOWN = 0, 1
NEAR, FAR = 0, 1


def kernel(
    planes,
    peers,
    q_hbm,
    k_hbm,
    v_hbm,
    out_ref,
    q_ref,
    kv_ref,
    best_ref,
    acc_ref,
    stage_ref,
    load_sem,
    x_sem,
    ring_send,
    ring_recv,
    core_send,
    core_recv,
    out_send,
    out_recv,
    own_sem,
):
    rows, width = q_ref.shape
    heads = width // HD
    groups = heads // UNROLL
    part = rows // peers
    reach = planes // 2
    me = lax.axis_index("ctx")
    tp = lax.axis_index("tp")
    z, x, core = me // PLANE, (me // 2) % 2, me % 2

    def slot(plane, col, c):
        return plane * PLANE + (x if col == NEAR else 1 - x) * 2 + c

    def beside(d, step):
        return lax.rem(z + planes - step if d == UP else z + step, planes)

    neighbour = (
        lax.rem(z + 1, planes) * PLANE + x * 2 + core,
        lax.rem(z + planes - 1, planes) * PLANE + x * 2 + core,
    )
    x_partner = z * PLANE + (1 - x) * 2 + core
    core_partner = z * PLANE + x * 2 + 1 - core

    def last(d, col):
        return reach if (d == UP) == (col == NEAR) else reach - 1

    def needed(d, step, at):
        return at >= step if d == UP else at + step >= planes

    def carried(d, col, step, at):
        if d == UP:
            return needed(d, step, at)
        return needed(d, step, at) | (at + step + 1 <= last(d, col))

    def passes(d, col, step):
        at = lax.rem(z + 1 if d == UP else z + planes - 1, planes)
        return (step < last(d, col)) & carried(d, col, step + 1, at)

    def remote(index, send, recv, target):
        return pltpu.make_async_remote_copy(
            src_ref=kv_ref.at[index],
            dst_ref=kv_ref.at[index],
            send_sem=send,
            recv_sem=recv,
            device_id={"ctx": target},
            device_id_type=MESH,
        )

    def hop(d, col, step):
        return remote(
            slot(beside(d, step), col, core),
            ring_send.at[d, col, step],
            ring_recv.at[d, col, step + 1],
            neighbour[d],
        )

    def across(d, col, step, c):
        return remote(
            slot(beside(d, step), col, c),
            core_send.at[d, col, step],
            core_recv.at[d, col, step],
            core_partner,
        )

    def arrive(d, col, step):
        remote(
            slot(beside(d, step), col, core),
            ring_send.at[d, col, step],
            ring_recv.at[d, col, step],
            neighbour[d],
        ).wait_recv()

        @pl.when(passes(d, col, step))
        def _():
            hop(d, col, step).start()

        @pl.when(needed(d, step, z))
        def _():
            across(d, col, step, core).start()

    def arrive_both(col, step):
        for d in (UP, DOWN):

            @pl.when((step <= last(d, col)) & carried(d, col, step, z))
            def _():
                arrive(d, col, step)

    def begin(col):
        for d in (UP, DOWN):

            @pl.when(passes(d, col, 0))
            def _():
                hop(d, col, 0).start()

        across(UP, col, 0, core).start()

    def whole(d, step):
        @pl.when(needed(d, step, z))
        def _():
            for col in (NEAR, FAR):
                across(d, col, step, 1 - core).wait_recv()

    loads = [
        pltpu.make_async_copy(k_hbm, kv_ref.at[me, 0], load_sem.at[0]),
        pltpu.make_async_copy(v_hbm, kv_ref.at[me, 1], load_sem.at[1]),
        pltpu.make_async_copy(q_hbm, q_ref, load_sem.at[2]),
    ]
    for load in loads:
        load.start()
    barrier = pltpu.get_barrier_semaphore()
    for target in (*neighbour, x_partner, core_partner):
        pl.semaphore_signal(barrier, inc=1, device_id={"ctx": target}, device_id_type=MESH)
    for j in range(1, peers):
        pl.semaphore_signal(
            barrier, inc=1, device_id={"tp": lax.rem(tp + j, peers)}, device_id_type=MESH
        )
    loads[0].wait()
    loads[1].wait()
    pl.semaphore_wait(barrier, 4 + peers - 1)

    x_copy = remote(me, x_sem.at[0], x_sem.at[1], x_partner)
    x_copy.start()
    begin(NEAR)
    best_ref[...] = jnp.full_like(best_ref, -1e30)
    acc_ref[...] = jnp.zeros_like(acc_ref)

    def attend(first, count, group, masked):
        held = kv_ref.at[pl.ds(first, count)]
        block_rows = count * rows
        key = held[:, 0].reshape(block_rows, HD)
        value = jnp.concatenate(
            [held[:, 1].reshape(block_rows, HD), jnp.ones((block_rows, HD), jnp.bfloat16)], axis=1
        )
        for u in range(UNROLL):
            head = group * UNROLL + u
            q = q_ref[:, pl.ds(pl.multiple_of(head * HD, HD), HD)]
            s = lax.dot_general(q, key, (((1,), (1,)), ((), ())), preferred_element_type=jnp.float32)
            if masked:
                row = (me - first) * rows + lax.broadcasted_iota(jnp.int32, s.shape, 0)
                col = lax.broadcasted_iota(jnp.int32, s.shape, 1)
                s = jnp.where(col <= row, s, -1e30)
            old = best_ref[head]
            new = jnp.maximum(old, jnp.max(s, axis=1, keepdims=True))
            fade = jnp.exp2((old - new) * SCALE)
            p = jnp.exp2((s - new[:, :1]) * SCALE).astype(jnp.bfloat16)
            pv = jnp.dot(p, value, preferred_element_type=jnp.float32)
            acc_ref[head] = acc_ref[head] * jnp.concatenate([fade, fade], axis=1) + pv
            best_ref[head] = new

    def near(group, carry):
        @pl.when(group == groups - 1)
        def _():
            arrive_both(NEAR, 1)

        attend(me - core, 2, group, True)
        return carry

    def far(group, carry):
        @pl.when(group == groups - 1)
        def _():
            arrive_both(FAR, 1)

        @pl.when(x == 1)
        def _():
            attend(z * PLANE, 2, group, False)

        return carry

    across(UP, NEAR, 0, 1 - core).wait_recv()
    loads[2].wait()
    lax.fori_loop(0, groups, near, 0)
    remote(x_partner, x_sem.at[0], x_sem.at[1], x_partner).wait_recv()
    begin(FAR)
    arrive_both(NEAR, 2)
    across(UP, FAR, 0, 1 - core).wait_recv()
    lax.fori_loop(0, groups, far, 0)

    def attend_step(step, carry):
        def attend_side(d, carry):
            @pl.when(d == 0)
            def _():
                arrive_both(NEAR, step + 2)
                whole(UP, step)

            @pl.when(d == 1)
            def _():
                whole(DOWN, step)

            plane = lax.rem(z + planes + (2 * d - 1) * step, planes)

            def each(group, carry):
                @pl.when((d == 0) & (group == groups - 1))
                def _():
                    arrive_both(FAR, step + 1)

                @pl.when(plane < z)
                def _():
                    attend(plane * PLANE, PLANE, group, False)

                return carry

            return lax.fori_loop(0, groups, each, carry)

        return lax.fori_loop(0, 2, attend_side, carry)

    lax.fori_loop(1, reach, attend_step, 0)

    @pl.when(z >= reach)
    def _():
        across(UP, NEAR, reach, 1 - core).wait_recv()
        across(DOWN, FAR, reach, 1 - core).wait_recv()

    cut = UNROLL * HD

    def give(group, j, to, column):
        return pltpu.make_async_remote_copy(
            src_ref=stage_ref.at[
                pl.ds(pl.multiple_of(to * part, part), part),
                pl.ds(pl.multiple_of(group * cut, cut), cut),
            ],
            dst_ref=out_ref.at[:, pl.ds(pl.multiple_of(column * width + group * cut, cut), cut)],
            send_sem=out_send.at[group, j],
            recv_sem=out_recv.at[group, j],
            device_id={"tp": to},
            device_id_type=MESH,
        )

    def keep(group):
        return pltpu.make_async_copy(
            stage_ref.at[
                pl.ds(pl.multiple_of(tp * part, part), part),
                pl.ds(pl.multiple_of(group * cut, cut), cut),
            ],
            out_ref.at[:, pl.ds(pl.multiple_of(tp * width + group * cut, cut), cut)],
            own_sem.at[group],
        )

    def finish(group, carry):
        @pl.when(z >= reach)
        def _():
            attend((z - reach) * PLANE, PLANE, group, False)

        for u in range(UNROLL):
            head = group * UNROLL + u
            acc = acc_ref[head]
            stage_ref[:, pl.ds(pl.multiple_of(head * HD, HD), HD)] = (
                acc[:, :HD] / acc[:, HD:]
            ).astype(jnp.bfloat16)
        for j in range(1, peers):
            give(group, j, lax.rem(tp + j, peers), tp).start()
        keep(group).start()
        return carry

    lax.fori_loop(0, groups, finish, 0)

    x_copy.wait_send()
    for col in (NEAR, FAR):
        across(UP, col, 0, core).wait_send()
    for d in (UP, DOWN):
        for col in (NEAR, FAR):
            for step in range(last(d, col) + 1):
                @pl.when(passes(d, col, step))
                def _():
                    hop(d, col, step).wait_send()

                if step > 0:

                    @pl.when(needed(d, step, z))
                    def _():
                        across(d, col, step, core).wait_send()
    for group in range(groups):
        for j in range(1, peers):
            copy = give(group, j, lax.rem(tp + j, peers), lax.rem(tp + peers - j, peers))
            copy.wait_send()
            copy.wait_recv()
        keep(group).wait()


def local(planes, peers, queries, keys, values):
    _, rows, width = queries.shape
    heads = width // HD
    groups = heads // UNROLL
    steps = planes // 2 + 1
    dma = pltpu.SemaphoreType.DMA
    out = pl.pallas_call(
        functools.partial(kernel, planes, peers),
        out_shape=jax.ShapeDtypeStruct((rows // peers, width * peers), jnp.bfloat16),
        in_specs=[pl.BlockSpec(memory_space=pltpu.HBM)] * 3,
        out_specs=pl.BlockSpec(memory_space=pltpu.HBM),
        scratch_shapes=[
            pltpu.VMEM((rows, width), jnp.bfloat16),
            pltpu.VMEM((planes * PLANE, 2, rows, HD), jnp.bfloat16),
            pltpu.VMEM((heads, rows, HD), jnp.float32),
            pltpu.VMEM((heads, rows, 2 * HD), jnp.float32),
            pltpu.VMEM((rows, width), jnp.bfloat16),
            dma((3,)),
            dma((2,)),
            dma((2, 2, steps)),
            dma((2, 2, steps)),
            dma((2, 2, steps)),
            dma((2, 2, steps)),
            dma((groups, peers)),
            dma((groups, peers)),
            dma((groups,)),
        ],
        compiler_params=pltpu.CompilerParams(
            vmem_limit_bytes=67043328, collective_id=0, has_side_effects=True
        ),
        name="ring_attention",
    )(queries[0], keys[0], values[0])
    return out[None]


def solution(mesh):
    in_specs = (P(None, "ctx", "tp"), P(None, "ctx", "tp"), P(None, "ctx", "tp"))
    out_specs = P(None, ("ctx", "tp"), None)
    planes, peers = mesh.shape["ctx"] // PLANE, mesh.shape["tp"]
    return jax.shard_map(
        functools.partial(local, planes, peers),
        mesh=mesh,
        in_specs=in_specs,
        out_specs=out_specs,
        check_vma=False,
    )
```

```python
import functools
import math

import jax
import jax.numpy as jnp
from jax import lax
from jax.experimental import pallas as pl
from jax.experimental.pallas import tpu as pltpu
from jax.sharding import PartitionSpec as P

HD = 128
UNROLL = 4
SCALE = math.log2(math.e) / math.sqrt(HD)
MESH = pl.DeviceIdType.MESH

PLANE = 4
UP, DOWN = 0, 1
NEAR, FAR = 0, 1


def kernel(
    planes,
    peers,
    q_hbm,
    k_hbm,
    v_hbm,
    out_ref,
    q_ref,
    kv_ref,
    best_ref,
    acc_ref,
    stage_ref,
    load_sem,
    x_sem,
    ring_send,
    ring_recv,
    core_send,
    core_recv,
    out_send,
    out_recv,
    own_sem,
):
    rows, width = q_ref.shape
    heads = width // HD
    groups = heads // UNROLL
    part = rows // peers
    reach = planes // 2
    me = lax.axis_index("ctx")
    tp = lax.axis_index("tp")
    z, x, core = me // PLANE, (me // 2) % 2, me % 2

    def slot(plane, col, c):
        return plane * PLANE + (x if col == NEAR else 1 - x) * 2 + c

    def beside(d, step):
        return lax.rem(z + planes - step if d == UP else z + step, planes)

    neighbour = (
        lax.rem(z + 1, planes) * PLANE + x * 2 + core,
        lax.rem(z + planes - 1, planes) * PLANE + x * 2 + core,
    )
    x_partner = z * PLANE + (1 - x) * 2 + core
    core_partner = z * PLANE + x * 2 + 1 - core

    def last(d, col):
        return reach if (d == UP) == (col == NEAR) else reach - 1

    def needed(d, step, at):
        return at >= step if d == UP else at + step >= planes

    def carried(d, col, step, at):
        if d == UP:
            return needed(d, step, at)
        return needed(d, step, at) | (at + step + 1 <= last(d, col))

    def passes(d, col, step):
        at = lax.rem(z + 1 if d == UP else z + planes - 1, planes)
        return (step < last(d, col)) & carried(d, col, step + 1, at)

    def remote(index, send, recv, target):
        return pltpu.make_async_remote_copy(
            src_ref=kv_ref.at[index],
            dst_ref=kv_ref.at[index],
            send_sem=send,
            recv_sem=recv,
            device_id={"ctx": target},
            device_id_type=MESH,
        )

    def hop(d, col, step):
        return remote(
            slot(beside(d, step), col, core),
            ring_send.at[d, col, step],
            ring_recv.at[d, col, step + 1],
            neighbour[d],
        )

    def across(d, col, step, c):
        return remote(
            slot(beside(d, step), col, c),
            core_send.at[d, col, step],
            core_recv.at[d, col, step],
            core_partner,
        )

    def arrive(d, col, step):
        remote(
            slot(beside(d, step), col, core),
            ring_send.at[d, col, step],
            ring_recv.at[d, col, step],
            neighbour[d],
        ).wait_recv()

        @pl.when(passes(d, col, step))
        def _():
            hop(d, col, step).start()

        @pl.when(needed(d, step, z))
        def _():
            across(d, col, step, core).start()

    def arrive_both(col, step):
        for d in (UP, DOWN):

            @pl.when((step <= last(d, col)) & carried(d, col, step, z))
            def _():
                arrive(d, col, step)

    def begin(col):
        for d in (UP, DOWN):

            @pl.when(passes(d, col, 0))
            def _():
                hop(d, col, 0).start()

        across(UP, col, 0, core).start()

    def whole(d, step):
        @pl.when(needed(d, step, z))
        def _():
            for col in (NEAR, FAR):
                across(d, col, step, 1 - core).wait_recv()

    loads = [
        pltpu.make_async_copy(k_hbm, kv_ref.at[me, 0], load_sem.at[0]),
        pltpu.make_async_copy(v_hbm, kv_ref.at[me, 1], load_sem.at[1]),
        pltpu.make_async_copy(q_hbm, q_ref, load_sem.at[2]),
    ]
    for load in loads:
        load.start()
    barrier = pltpu.get_barrier_semaphore()
    for target in (*neighbour, x_partner, core_partner):
        pl.semaphore_signal(barrier, inc=1, device_id={"ctx": target}, device_id_type=MESH)
    for j in range(1, peers):
        pl.semaphore_signal(
            barrier, inc=1, device_id={"tp": lax.rem(tp + j, peers)}, device_id_type=MESH
        )
    loads[0].wait()
    loads[1].wait()
    pl.semaphore_wait(barrier, 4 + peers - 1)

    x_copy = remote(me, x_sem.at[0], x_sem.at[1], x_partner)
    x_copy.start()
    begin(NEAR)
    best_ref[...] = jnp.full_like(best_ref, -1e30)
    acc_ref[...] = jnp.zeros_like(acc_ref)

    def attend(first, count, group, masked):
        held = kv_ref.at[pl.ds(first, count)]
        block_rows = count * rows
        key = held[:, 0].reshape(block_rows, HD)
        value = jnp.concatenate(
            [held[:, 1].reshape(block_rows, HD), jnp.ones((block_rows, HD), jnp.bfloat16)], axis=1
        )
        for u in range(UNROLL):
            head = group * UNROLL + u
            q = q_ref[:, pl.ds(pl.multiple_of(head * HD, HD), HD)]
            s = lax.dot_general(q, key, (((1,), (1,)), ((), ())), preferred_element_type=jnp.float32)
            if masked:
                row = (me - first) * rows + lax.broadcasted_iota(jnp.int32, s.shape, 0)
                col = lax.broadcasted_iota(jnp.int32, s.shape, 1)
                s = jnp.where(col <= row, s, -1e30)
            old = best_ref[head]
            new = jnp.maximum(old, jnp.max(s, axis=1, keepdims=True))
            fade = jnp.exp2((old - new) * SCALE)
            p = jnp.exp2(s * SCALE - (new * SCALE)[:, :1]).astype(jnp.bfloat16)
            pv = jnp.dot(p, value, preferred_element_type=jnp.float32)
            acc_ref[head] = acc_ref[head] * jnp.concatenate([fade, fade], axis=1) + pv
            best_ref[head] = new

    def near(group, carry):
        @pl.when(group == groups - 1)
        def _():
            arrive_both(NEAR, 1)

        attend(me - core, 2, group, True)
        return carry

    def far(group, carry):
        @pl.when(group == groups - 1)
        def _():
            arrive_both(FAR, 1)

        @pl.when(x == 1)
        def _():
            attend(z * PLANE, 2, group, False)

        return carry

    across(UP, NEAR, 0, 1 - core).wait_recv()
    loads[2].wait()
    lax.fori_loop(0, groups, near, 0)
    remote(x_partner, x_sem.at[0], x_sem.at[1], x_partner).wait_recv()
    begin(FAR)
    arrive_both(NEAR, 2)
    across(UP, FAR, 0, 1 - core).wait_recv()
    lax.fori_loop(0, groups, far, 0)

    def attend_step(step, carry):
        def attend_side(d, carry):
            @pl.when(d == 0)
            def _():
                arrive_both(NEAR, step + 2)
                whole(UP, step)

            @pl.when(d == 1)
            def _():
                whole(DOWN, step)

            plane = lax.rem(z + planes + (2 * d - 1) * step, planes)

            def each(group, carry):
                @pl.when((d == 0) & (group == groups - 1))
                def _():
                    arrive_both(FAR, step + 1)

                @pl.when(plane < z)
                def _():
                    attend(plane * PLANE, PLANE, group, False)

                return carry

            return lax.fori_loop(0, groups, each, carry)

        return lax.fori_loop(0, 2, attend_side, carry)

    lax.fori_loop(1, reach, attend_step, 0)

    @pl.when(z >= reach)
    def _():
        across(UP, NEAR, reach, 1 - core).wait_recv()
        across(DOWN, FAR, reach, 1 - core).wait_recv()

    cut = UNROLL * HD

    def give(group, j, to, column):
        return pltpu.make_async_remote_copy(
            src_ref=stage_ref.at[
                pl.ds(pl.multiple_of(to * part, part), part),
                pl.ds(pl.multiple_of(group * cut, cut), cut),
            ],
            dst_ref=out_ref.at[:, pl.ds(pl.multiple_of(column * width + group * cut, cut), cut)],
            send_sem=out_send.at[group, j],
            recv_sem=out_recv.at[group, j],
            device_id={"tp": to},
            device_id_type=MESH,
        )

    def keep(group):
        return pltpu.make_async_copy(
            stage_ref.at[
                pl.ds(pl.multiple_of(tp * part, part), part),
                pl.ds(pl.multiple_of(group * cut, cut), cut),
            ],
            out_ref.at[:, pl.ds(pl.multiple_of(tp * width + group * cut, cut), cut)],
            own_sem.at[group],
        )

    def finish(group, carry):
        @pl.when(z >= reach)
        def _():
            attend((z - reach) * PLANE, PLANE, group, False)

        for u in range(UNROLL):
            head = group * UNROLL + u
            acc = acc_ref[head]
            stage_ref[:, pl.ds(pl.multiple_of(head * HD, HD), HD)] = (
                acc[:, :HD] / acc[:, HD:]
            ).astype(jnp.bfloat16)
        for j in range(1, peers):
            give(group, j, lax.rem(tp + j, peers), tp).start()
        keep(group).start()
        return carry

    lax.fori_loop(0, groups, finish, 0)

    x_copy.wait_send()
    for col in (NEAR, FAR):
        across(UP, col, 0, core).wait_send()
    for d in (UP, DOWN):
        for col in (NEAR, FAR):
            for step in range(last(d, col) + 1):
                @pl.when(passes(d, col, step))
                def _():
                    hop(d, col, step).wait_send()

                if step > 0:

                    @pl.when(needed(d, step, z))
                    def _():
                        across(d, col, step, core).wait_send()
    for group in range(groups):
        for j in range(1, peers):
            copy = give(group, j, lax.rem(tp + j, peers), lax.rem(tp + peers - j, peers))
            copy.wait_send()
            copy.wait_recv()
        keep(group).wait()


def local(planes, peers, queries, keys, values):
    _, rows, width = queries.shape
    heads = width // HD
    groups = heads // UNROLL
    steps = planes // 2 + 1
    dma = pltpu.SemaphoreType.DMA
    out = pl.pallas_call(
        functools.partial(kernel, planes, peers),
        out_shape=jax.ShapeDtypeStruct((rows // peers, width * peers), jnp.bfloat16),
        in_specs=[pl.BlockSpec(memory_space=pltpu.HBM)] * 3,
        out_specs=pl.BlockSpec(memory_space=pltpu.HBM),
        scratch_shapes=[
            pltpu.VMEM((rows, width), jnp.bfloat16),
            pltpu.VMEM((planes * PLANE, 2, rows, HD), jnp.bfloat16),
            pltpu.VMEM((heads, rows, HD), jnp.float32),
            pltpu.VMEM((heads, rows, 2 * HD), jnp.float32),
            pltpu.VMEM((rows, width), jnp.bfloat16),
            dma((3,)),
            dma((2,)),
            dma((2, 2, steps)),
            dma((2, 2, steps)),
            dma((2, 2, steps)),
            dma((2, 2, steps)),
            dma((groups, peers)),
            dma((groups, peers)),
            dma((groups,)),
        ],
        compiler_params=pltpu.CompilerParams(
            vmem_limit_bytes=67043328, collective_id=0, has_side_effects=True
        ),
        name="ring_attention",
    )(queries[0], keys[0], values[0])
    return out[None]


def solution(mesh):
    in_specs = (P(None, "ctx", "tp"), P(None, "ctx", "tp"), P(None, "ctx", "tp"))
    out_specs = P(None, ("ctx", "tp"), None)
    planes, peers = mesh.shape["ctx"] // PLANE, mesh.shape["tp"]
    return jax.shard_map(
        functools.partial(local, planes, peers),
        mesh=mesh,
        in_specs=in_specs,
        out_specs=out_specs,
        check_vma=False,
    )
```
